128 devices in a mesh: dec: 4 (over x_lo, core), ra: 32 (over x_hi, y, z).
Axes of the slice: x: 4 (x_hi: 2, x_lo: 2; x = x_hi * 2 + x_lo), y: 4, z: 4, core: 2. Of those that a mesh axis runs over, the one named last changes fastest.
Arguments:
- params: float32 [128, 44, 384], P(('dec', 'ra')), may hold values from -6 to 6
- mixing: float32 [44, 256], replicated, may hold values from -0.875 to 0.875
- basis: bfloat16 [256, 4096], replicated, may hold values from -0.375 to 0.375
- blend: float32 [128, 4, 64, 64], P(('dec', 'ra')), may hold values from -0.375 to 0.375
- border_ids: int32 [128, 64], P(('dec', 'ra')), may hold values from 0 to 383, as said below
- intersection: int32 [128, 384, 4], P(('dec', 'ra')), may hold values from 0 to 4, all different within a row; in each aligned block of 384 rows (0 to 383, 384 to 767, ..., all dimensions but the last counted through in order) at most 384 rows name the same one
- observed: bfloat16 [128, 5, 384, 4096], P(('dec', 'ra')), may hold values from -6 to 6
Outputs:
- gradient: float32 [128, 44, 384], P(('dec', 'ra'))
The draws below stay inside these ranges and needn't reach their ends.
Inputs may be any that keep to these rules, and one draw needn't show every extreme that they name: `intersection`: each source names 4 different offset indices; among the sources of one tile each index is named at most 384 times, and exactly 384 times in some tile. `border_ids`: 64 different sources of the tile.
All inputs are finite; a program needn't handle non-finite values.
Results may differ from the reference program's by a relative error of at most 0.0017.
Values may be sent and summed in bfloat16 or wider, within the bound.
A program may use at most 64 MiB of HBM per device.

```python
import math
import jax
import jax.numpy as jnp
import numpy as np
from jax import lax

P_SIZE = 44
K = 256
PIX = 4096
TOP = 4
HALF = 2
S_DEV = 384
NOFF = 5
NB = 64
CAP = 384
TILES = 128
N_DEC = 4
N_RA = 32


def draw_border_ids(key, part):
    tile_keys = jax.random.split(key, TILES)

    def one_tile(tile_key):
        return jax.random.permutation(tile_key, S_DEV)[:NB]
    return jax.vmap(one_tile)(tile_keys).astype(jnp.int32)


def levels(key, shape, cuts, least, largest):
    def one(position, parts):
        heights = jax.random.uniform(jax.random.fold_in(jax.random.fold_in(key, 6), position), (parts,), jnp.float32, least / len(cuts), largest / len(cuts))
        return jnp.repeat(jnp.exp(heights), shape[position] // parts).reshape((-1,) + (1,) * (len(shape) - position - 1))

    loudness = one(*cuts[0])
    for cut in cuts[1:]:
        loudness = loudness * one(*cut)
    return loudness


def routed_block(key, own, number, rows, count, top, most, lean):
    order = jax.random.permutation(key, count)
    crowded, common = shares(count, rows * top, most, lean, True), shares(count, rows * top, most, lean, False)
    places = jnp.arange(count)

    def named(lengths, rotation):
        used = int((lengths > 0).sum())
        fixed = max(1, used // 4)
        moved = fixed + (places - fixed + rotation * (used - fixed)) % max(1, count - fixed)
        return jnp.zeros((count,), jnp.int32).at[order[jnp.where(places < fixed, places, moved)]].set(jnp.asarray(lengths, jnp.int32))

    lengths = jnp.where(number % 4 == 0, named(crowded, number // 4), named(common, number - number // 4 - 1))
    mixed = jax.random.permutation(jax.random.fold_in(own, 3), count)
    giver, receiver = mixed[0:count // 2 * 2:2], mixed[1:count // 2 * 2:2]
    margin = jnp.minimum(lengths[giver] - 1, most - lengths[receiver]) // 2
    margin = jnp.where((giver == order[0]) | (receiver == order[0]) | (lengths[receiver] == 0), 0, jnp.maximum(margin, 0))
    moved = jax.random.randint(jax.random.fold_in(own, 4), (count // 2,), 0, 1 << 20) % (margin + 1)
    lengths = lengths.at[giver].add(-moved).at[receiver].add(moved)
    labels = jnp.searchsorted(jnp.cumsum(lengths), jnp.arange(rows * top), side="right").astype(jnp.int32)
    table = labels.reshape(top, rows).T
    table = table[jax.random.permutation(jax.random.fold_in(own, 1), rows)]
    rotation = jax.random.randint(jax.random.fold_in(own, 2), (rows, 1), 0, top)
    return jnp.take_along_axis(table, (jnp.arange(top)[None, :] + rotation) % top, axis=1)


def shares(amount, total, reach, skew, full):
    loads = [(1 << 20) // math.isqrt(rank ** skew) + 1 for rank in range(1, amount + 1)]
    largest = reach if full else min(reach, max(-(-total // amount), total * loads[0] // sum(loads)))
    least = 1 if total - largest >= amount - 1 else 0
    holding, surplus = [largest] + [least] * (amount - 1), total - largest - least * (amount - 1)
    while surplus > 0:
        candidates = [i for i in range(1, amount) if holding[i] < largest] or [i for i in range(1, amount) if holding[i] < reach]
        whole, remaining = sum([loads[i] for i in candidates]), surplus
        for i in candidates:
            more = min(reach - holding[i], max(1, remaining * loads[i] // whole), surplus)
            holding[i] = holding[i] + more
            surplus = surplus - more
    return np.array(holding)


def bell_draw(rng, dims, width, reach, pieces=(), kind=jnp.bfloat16):
    drawn = width * jax.random.normal(rng, dims, jnp.float32)
    if pieces:
        drawn = drawn * levels(rng, dims, pieces, -0.22, 0.18)
    return jnp.clip(drawn, -reach, reach).astype(kind)


def setup_inputs(seed: int = 0) -> dict:
    streams_of = jax.random.split(jax.random.key(seed), 8)
    params = bell_draw(streams_of[0], (TILES, P_SIZE, S_DEV), 1.0, 6.0, ((0, 128),), jnp.float32)
    mixing = bell_draw(streams_of[1], (P_SIZE, K), P_SIZE ** -0.5, 0.875, (), jnp.float32)
    basis = bell_draw(streams_of[2], (K, PIX), K ** -0.5, 0.375)
    blend = bell_draw(streams_of[3], (TILES, 4, NB, NB), (4 * NB) ** -0.5, 0.375, ((0, 128),), jnp.float32)
    border_ids = draw_border_ids(jax.random.fold_in(streams_of[7], 71), 0)
    intersection_keys = jax.random.split(jax.random.fold_in(streams_of[5], 1), TILES * S_DEV // S_DEV)
    intersection_turns = jax.random.permutation(jax.random.fold_in(streams_of[5], 3), TILES * S_DEV // S_DEV)
    intersection = jax.vmap(lambda own, number: routed_block(jax.random.fold_in(streams_of[5], 2), own, number, S_DEV, NOFF, TOP, CAP, 2))(intersection_keys, intersection_turns).reshape((TILES, S_DEV, TOP))
    observed = bell_draw(streams_of[6], (TILES, NOFF, CAP, PIX), 1.0, 6.0, ((0, 128),))
    return {"params": params, "mixing": mixing, "basis": basis, "blend": blend, "border_ids": border_ids, "intersection": intersection, "observed": observed}


HIGHEST_PREC = lax.Precision.HIGHEST

def add_rows(table, where_rows, extra):
    return table.at[where_rows].add(extra)

def take_rows(table, where_rows):
    return table[where_rows]

def reference(params, mixing, basis, blend, border_ids, intersection, observed):
    logits = jnp.einsum('tps,pk->tsk', params, mixing, precision=HIGHEST_PREC)
    amplitudes = jax.nn.softplus(logits)
    rim_amps = jax.vmap(take_rows)(amplitudes, border_ids)
    grid_rim = rim_amps.reshape(N_DEC, N_RA, NB, K)
    empty_band = jnp.zeros((1, N_RA, NB, K), jnp.float32)
    below_rim = jnp.concatenate([empty_band, grid_rim[:-1]], axis=0)
    above_rim = jnp.concatenate([grid_rim[1:], empty_band], axis=0)
    west_rim = jnp.roll(grid_rim, 1, axis=1)
    east_rim = jnp.roll(grid_rim, -1, axis=1)
    nearby = jnp.stack([below_rim, above_rim, west_rim, east_rim], axis=2).reshape(TILES, 4, NB, K)
    light_in = jnp.einsum('tsij,tsjk->tik', blend, nearby, precision=HIGHEST_PREC)
    blended = jax.vmap(add_rows)(amplitudes, border_ids, light_in)
    sent_amps = blended.astype(jnp.bfloat16)
    flat_owner = intersection.reshape(TILES, S_DEV * TOP)
    onehot = (flat_owner[:, :, None] == jnp.arange(NOFF, dtype=jnp.int32)[None, None, :]).astype(jnp.int32)
    before = jnp.cumsum(onehot, axis=1) - onehot
    slot_index = lax.optimization_barrier(jnp.sum(onehot * before, axis=2))
    dest_row = (flat_owner * CAP + slot_index).astype(jnp.int32)
    source_row = jnp.arange(S_DEV * TOP, dtype=jnp.int32) // TOP

    def pack_tile(tile_amps, tile_dest):
        return jnp.zeros((NOFF * CAP, K), jnp.bfloat16).at[tile_dest].set(tile_amps[source_row])
    packets = jax.vmap(pack_tile)(sent_amps, dest_row).reshape(N_DEC, N_RA, NOFF, CAP, K)
    arrived = jnp.stack([jnp.roll(packets[:, :, offset_id], offset_id - HALF, axis=1) for offset_id in range(NOFF)], axis=2)
    pix_scale = 1.0 / math.sqrt(PIX)

    def render_tile(pair):
        packed, seen = pair
        rendered = jnp.dot(packed, basis, preferred_element_type=jnp.float32)
        residual = (rendered - seen.astype(jnp.float32)).astype(jnp.bfloat16)
        pulled = jnp.dot(residual, basis.T, preferred_element_type=jnp.float32)
        return (pulled * pix_scale).astype(jnp.bfloat16)
    pulled_all = lax.map(render_tile, (arrived.reshape(TILES, NOFF * CAP, K), observed.reshape(TILES, NOFF * CAP, PIX)))
    pulled_grid = pulled_all.reshape(N_DEC, N_RA, NOFF, CAP, K)
    returned = jnp.stack([jnp.roll(pulled_grid[:, :, offset_id], HALF - offset_id, axis=1) for offset_id in range(NOFF)], axis=2)
    returned = returned.reshape(TILES, NOFF * CAP, K)
    gathered = jax.vmap(take_rows)(returned, dest_row).astype(jnp.float32)
    grad_sent = lax.optimization_barrier(jnp.sum(gathered.reshape(TILES, S_DEV, TOP, K), axis=2))
    rim_grad = jax.vmap(take_rows)(grad_sent, border_ids)
    toward = jnp.einsum('tsij,tik->tsjk', blend, rim_grad, precision=HIGHEST_PREC).reshape(N_DEC, N_RA, 4, NB, K)
    from_above = jnp.concatenate([toward[1:, :, 0], empty_band], axis=0)
    from_below = jnp.concatenate([empty_band, toward[:-1, :, 1]], axis=0)
    from_east = jnp.roll(toward[:, :, 2], -1, axis=1)
    from_west = jnp.roll(toward[:, :, 3], 1, axis=1)
    incoming = (from_above + from_below + from_east + from_west).reshape(TILES, NB, K)
    grad_amps = jax.vmap(add_rows)(grad_sent, border_ids, incoming)
    gradient = jnp.einsum('pk,tsk->tps', mixing, grad_amps * jax.nn.sigmoid(logits), precision=HIGHEST_PREC)
    return gradient
```

```python
import math

import jax
import jax.numpy as jnp
from jax import lax
from jax.experimental import pallas as pl
from jax.experimental.pallas import tpu as pltpu
from jax.sharding import PartitionSpec as P

HIGH = lax.Precision.HIGHEST
MESH = pl.DeviceIdType.MESH
F32, BF16 = jnp.float32, jnp.bfloat16


def dot(a, b, da, db, precision=None):
    return lax.dot_general(
        a, b, (((da,), (db,)), ((), ())), precision=precision, preferred_element_type=F32
    )


def kernel(
    params_ref, mixing_ref, blend_ref, ids_ref, owners_ref, basis_hbm, seen_hbm, out_ref,
    seen, basis, amps, sig, back_out, back_in, rim_out, rim_in, w_out, w_in,
    seen_sem, basis_sem, back_ssem, back_rsem, rim_ssem, rim_rsem, w_ssem, w_rsem,
):
    noff, cap, pix = seen.shape
    reach = noff // 2
    rows, top = owners_ref.shape
    border = ids_ref.shape[1]
    scale = 1.0 / math.sqrt(pix)
    nd, nr = lax.axis_size("dec"), lax.axis_size("ra")
    dec, ra = lax.axis_index("dec"), lax.axis_index("ra")

    def at_ra(step):
        return (dec, lax.rem(ra + step + nr, nr))

    def at_dec(step):
        return (lax.rem(dec + step + nd, nd), ra)

    def turn(step):
        return jnp.where(lax.rem(step, 2) == 0, step // 2, noff - 1 - step // 2)

    def seen_copy(j):
        return pltpu.make_async_copy(seen_hbm.at[j], seen.at[j], seen_sem.at[j])

    def back_copy(j, step):
        return pltpu.make_async_remote_copy(
            src_ref=back_out.at[j], dst_ref=back_in.at[j],
            send_sem=back_ssem.at[j], recv_sem=back_rsem.at[j],
            device_id=at_ra(step), device_id_type=MESH,
        )

    def rim_copy(slot, where):
        return pltpu.make_async_remote_copy(
            src_ref=rim_out, dst_ref=rim_in.at[slot],
            send_sem=rim_ssem.at[slot], recv_sem=rim_rsem.at[slot],
            device_id=where, device_id_type=MESH,
        )

    def w_copy(slot, where):
        return pltpu.make_async_remote_copy(
            src_ref=w_out.at[slot], dst_ref=w_in.at[slot],
            send_sem=w_ssem.at[slot], recv_sem=w_rsem.at[slot],
            device_id=where, device_id_type=MESH,
        )

    basis_copy = pltpu.make_async_copy(basis_hbm, basis, basis_sem)
    basis_copy.start()
    for j in (0, 4, 1, 3, 2):
        seen_copy(j).start()

    barrier = pltpu.get_barrier_semaphore()
    peers = [at_dec(1), at_dec(-1)]
    for step in range(1, reach + 1):
        peers += [at_ra(step), at_ra(-step)]
    for peer in peers:
        pl.semaphore_signal(barrier, inc=1, device_id=peer, device_id_type=MESH)

    logits = dot(params_ref[...], mixing_ref[...], 0, 0, HIGH)
    decay = jnp.exp(-jnp.abs(logits))
    amps[...] = jnp.maximum(logits, 0.0) + jnp.log1p(decay)
    sig[...] = jnp.where(logits >= 0, 1.0, decay) / (1.0 + decay)
    pick = (lax.broadcasted_iota(jnp.int32, (rows, border), 0) == ids_ref[...]).astype(F32)
    rim_out[...] = dot(pick, amps[...], 0, 0, HIGH)

    pl.semaphore_wait(barrier, len(peers))
    rim_copies = [
        rim_copy(0, at_dec(1)), rim_copy(1, at_dec(-1)), rim_copy(2, at_ra(1)), rim_copy(3, at_ra(-1)),
    ]
    for copy in rim_copies:
        copy.start()

    basis_copy.wait()

    def render(step, carry):
        j = turn(step)
        seen_copy(j).wait()
        back_out[j] = (dot(seen[j], basis[...], 1, 1) * scale).astype(BF16)
        return carry

    def render_and_send(step, carry):
        render(step, carry)
        j = turn(step)
        back_copy(j, reach - j).start()
        return carry

    lax.fori_loop(0, noff - 1, render_and_send, 0)
    render(noff - 1, 0)

    gram = dot(basis[...], basis[...], 1, 1)
    gram_hi = gram.astype(BF16)
    gram_lo = (gram - gram_hi.astype(F32)).astype(BF16)

    for copy in rim_copies:
        copy.wait_recv()
    light = jnp.zeros((border, amps.shape[1]), F32)
    masks = (dec > 0, dec < nd - 1, None, None)
    for side in range(4):
        part = dot(blend_ref[side], rim_in[side], 1, 0, HIGH)
        light = light + (part if masks[side] is None else jnp.where(masks[side], part, 0.0))
    sent = (amps[...] + dot(pick, light, 1, 0, HIGH)).astype(BF16)
    base = (dot(sent, gram_hi, 1, 0) + dot(sent, gram_lo, 1, 0)) * (top * scale)

    total = noff * (noff - 1) // 2
    missing = total - jnp.sum(owners_ref[...], axis=1, keepdims=True)
    lanes = lax.broadcasted_iota(jnp.int32, (rows, 128), 1)
    member = (missing != lanes).astype(F32).astype(BF16)
    earlier = (
        lax.broadcasted_iota(jnp.int32, (rows, rows), 1)
        < lax.broadcasted_iota(jnp.int32, (rows, rows), 0)
    ).astype(F32).astype(BF16)
    slots = dot(earlier, member, 1, 0).astype(jnp.int32)
    places = lax.broadcasted_iota(jnp.int32, (rows, cap), 1)

    def unpacked(j, block):
        slot = jnp.where(missing != j, slots[:, j : j + 1], -1)
        chosen = (slot == places).astype(F32).astype(BF16)
        return dot(chosen, block, 1, 0)

    grad = base - unpacked(reach, back_out[reach])
    for j in (0, 4, 1, 3):
        back_copy(j, reach - j).wait_recv()
        grad = grad - unpacked(j, back_in[j])

    rim_grad = dot(pick, grad, 0, 0, HIGH)
    w_copies = [
        w_copy(0, at_dec(-1)), w_copy(1, at_dec(1)), w_copy(2, at_ra(-1)), w_copy(3, at_ra(1)),
    ]
    for side in (2, 3, 0, 1):
        toward = dot(blend_ref[side], rim_grad, 0, 0, HIGH)
        slope = 1.0 - jnp.exp(-rim_in[side])
        w_out[side] = dot(mixing_ref[...], toward * slope, 1, 1, HIGH)
        w_copies[side].start()
    out = dot(mixing_ref[...], grad * sig[...], 1, 1, HIGH)
    for copy in w_copies:
        copy.wait_recv()
    w = (
        jnp.where(dec < nd - 1, w_in[0], 0.0) + jnp.where(dec > 0, w_in[1], 0.0) + w_in[2] + w_in[3]
    )
    out_ref[...] = out + dot(w, pick, 1, 1, HIGH)
    for copy in rim_copies + w_copies:
        copy.wait_send()
    for j in (0, 4, 1, 3):
        back_copy(j, reach - j).wait_send()


def local(params, mixing, basis, blend, border_ids, intersection, observed):
    p_size, rows = params.shape[1:]
    k = mixing.shape[1]
    noff, cap, pix = observed.shape[1:]
    border = border_ids.shape[1]
    vmem = pl.BlockSpec(memory_space=pltpu.VMEM)
    hbm = pl.BlockSpec(memory_space=pl.ANY)
    dma = pltpu.SemaphoreType.DMA
    out = pl.pallas_call(
        kernel,
        out_shape=jax.ShapeDtypeStruct((p_size, rows), F32),
        in_specs=[vmem] * 5 + [hbm] * 2,
        out_specs=vmem,
        scratch_shapes=[
            pltpu.VMEM((noff, cap, pix), BF16),
            pltpu.VMEM((k, pix), BF16),
            pltpu.VMEM((rows, k), F32),
            pltpu.VMEM((rows, k), F32),
            pltpu.VMEM((noff, cap, k), BF16),
            pltpu.VMEM((noff, cap, k), BF16),
            pltpu.VMEM((border, k), F32),
            pltpu.VMEM((4, border, k), F32),
            pltpu.VMEM((4, p_size, border), F32),
            pltpu.VMEM((4, p_size, border), F32),
            dma((noff,)), dma, dma((noff,)), dma((noff,)), dma((4,)), dma((4,)), dma((4,)), dma((4,)),
        ],
        compiler_params=pltpu.CompilerParams(
            collective_id=0, has_side_effects=True, vmem_limit_bytes=48 * 1024 * 1024
        ),
        name="tiles",
    )(params[0], mixing, blend[0], border_ids, intersection[0], basis, observed[0])
    return out[None]


def solution(mesh):
    in_specs = (
        P(("dec", "ra"), None, None),
        P(),
        P(),
        P(("dec", "ra"), None, None, None),
        P(("dec", "ra"), None),
        P(("dec", "ra"), None, None),
        P(("dec", "ra"), None, None, None),
    )
    out_specs = P(("dec", "ra"), None, None)
    return jax.shard_map(local, mesh=mesh, in_specs=in_specs, out_specs=out_specs, check_vma=False)
```

```python
import math

import jax
import jax.numpy as jnp
from jax import lax
from jax.experimental import pallas as pl
from jax.experimental.pallas import tpu as pltpu
from jax.sharding import PartitionSpec as P

HIGH = lax.Precision.HIGHEST
MESH = pl.DeviceIdType.MESH
F32, BF16 = jnp.float32, jnp.bfloat16


def dot(a, b, da, db, precision=None):
    return lax.dot_general(
        a, b, (((da,), (db,)), ((), ())), precision=precision, preferred_element_type=F32
    )


def halves(x):
    high = x.astype(BF16)
    return high, (x - high.astype(F32)).astype(BF16)


def onehot(hit):
    return hit.astype(F32).astype(BF16)


def kernel(
    params_hbm, mixing_hbm, blend_hbm, ids_hbm, owners_hbm, basis_hbm, seen_hbm, out_ref,
    params_ref, mixing_ref, blend_ref, ids_ref, owners_ref, mix2, fwd_params, fwd_slots,
    seen, basis, packed, placed, q_out, q_in, z_out, z_in, rim_out, rim_in, w_out, w_in,
    in_sem, seen_sem, basis_sem, slots_ssem, slots_rsem, params_ssem, params_rsem,
    q_ssem, q_rsem, z_ssem, z_rsem, rim_ssem, rim_rsem, w_ssem, w_rsem,
):
    noff, cap, pix = seen.shape
    mid = noff // 2
    top, rows = owners_ref.shape
    border = ids_ref.shape[1]
    p_size = params_ref.shape[0]
    half = mix2.shape[0] // 2
    scale = 1.0 / math.sqrt(pix)
    share = top * scale
    nd, nr = lax.axis_size("dec"), lax.axis_size("ra")
    dec, ra = lax.axis_index("dec"), lax.axis_index("ra")
    others = [j for j in range(noff) if j != mid]

    def at_ra(step):
        return (dec, lax.rem(ra + step + nr, nr))

    def at_dec(step):
        return (lax.rem(dec + step + nd, nd), ra)

    def turn(step):
        return jnp.where(step < mid, step, jnp.where(step < noff - 1, step + 1, mid))

    def seen_copy(j):
        return pltpu.make_async_copy(seen_hbm.at[j], seen.at[j], seen_sem.at[j])

    def remote(src, dst, ssem, rsem, where):
        return pltpu.make_async_remote_copy(
            src_ref=src, dst_ref=dst, send_sem=ssem, recv_sem=rsem,
            device_id=where, device_id_type=MESH,
        )

    def slots_copy(j):
        return remote(
            fwd_slots.at[mid], fwd_slots.at[j], slots_ssem.at[j], slots_rsem.at[j], at_ra(j - mid)
        )

    def params_copy(j):
        return remote(
            fwd_params.at[mid], fwd_params.at[j], params_ssem.at[j], params_rsem.at[j], at_ra(j - mid)
        )

    def q_copy(j):
        return remote(q_out.at[j], q_in.at[j], q_ssem.at[j], q_rsem.at[j], at_ra(mid - j))

    def z_copy(j):
        return remote(z_out.at[j], z_in.at[j], z_ssem.at[j], z_rsem.at[j], at_ra(mid - j))

    def mixed(x, full=True):
        high, low = halves(x)
        both = dot(mix2[...], high, 1, 1)
        out = both[:p_size] + both[half : half + p_size]
        return out + dot(mix2[:half], low, 1, 1)[:p_size] if full else out

    in_copies = [
        pltpu.make_async_copy(src, dst, in_sem.at[n])
        for n, (src, dst) in enumerate((
            (ids_hbm, ids_ref), (owners_hbm, owners_ref), (params_hbm.at[:, 0, :], params_ref),
            (mixing_hbm, mixing_ref), (blend_hbm, blend_ref),
        ))
    ]
    for copy in in_copies:
        copy.start()
    basis_copy = pltpu.make_async_copy(basis_hbm, basis, basis_sem)
    basis_copy.start()
    seen_copy(0).start()

    barrier = pltpu.get_barrier_semaphore()
    peers = [at_dec(1), at_dec(-1)] + [at_ra(j - mid) for j in others]
    for peer in peers:
        pl.semaphore_signal(barrier, inc=1, device_id=peer, device_id_type=MESH)

    earlier = onehot(
        lax.broadcasted_iota(jnp.int32, (rows, rows), 0)
        < lax.broadcasted_iota(jnp.int32, (rows, rows), 1)
    )
    mix2[...] = jnp.zeros_like(mix2)
    for copy in in_copies:
        copy.wait()
    seen_copy(1).start()
    pick = onehot(lax.broadcasted_iota(jnp.int32, (rows, border), 0) == ids_ref[...])
    spare = noff * (noff - 1) // 2 - jnp.sum(owners_ref[...], axis=0, keepdims=True)
    member = spare != lax.broadcasted_iota(jnp.int32, (8, rows), 0)
    slots = jnp.where(member, dot(onehot(member), earlier, 1, 0), -1.0)
    slots_hi, slots_lo = halves(slots)
    fwd_slots[mid, :, :rows] = slots
    fwd_slots[mid, :, rows : rows + border] = dot(slots_hi, pick, 1, 0) + dot(slots_lo, pick, 1, 0)
    fwd_slots[mid, :, rows + border :] = jnp.full((8, fwd_slots.shape[2] - rows - border), -1.0, F32)
    params = params_ref[...]
    mixing = mixing_ref[...]
    mix_hi, mix_lo = halves(mixing)
    mix2[:p_size] = mix_hi
    mix2[half : half + p_size] = mix_lo
    fwd_params[mid] = params.astype(BF16)
    rim_params = dot(params, pick.astype(F32), 1, 0, HIGH)
    rim_logits = dot(rim_params, mixing, 0, 0, HIGH)
    rim_decay = jnp.exp(-jnp.abs(rim_logits))
    rim_out[...] = jnp.maximum(rim_logits, 0.0) + jnp.log1p(rim_decay)

    pl.semaphore_wait(barrier, len(peers))
    for j in others:
        slots_copy(j).start()
    for j in others:
        params_copy(j).start()
    rim_copies = [
        remote(rim_out, rim_in.at[slot], rim_ssem.at[slot], rim_rsem.at[slot], where)
        for slot, where in enumerate((at_dec(1), at_dec(-1), at_ra(1), at_ra(-1)))
    ]
    for copy in rim_copies:
        copy.start()

    basis_copy.wait()

    def render(step, carry):
        j = turn(step)
        seen_copy(j).wait()

        @pl.when(step + 2 < noff)
        def _():
            seen_copy(turn(step + 2)).start()

        packed[j] = (dot(seen[j], basis[...], 1, 1) * scale).astype(BF16)
        return carry

    lax.fori_loop(0, noff, render, 0)

    places = lax.broadcasted_iota(jnp.int32, (rows + border, cap), 1).astype(F32)

    def place(j):
        column = fwd_slots[j].T[: rows + border, j : j + 1]
        block = dot(onehot(column == places), packed[j], 1, 0)
        return block[:rows], block[rows:]

    for j in others:
        slots_copy(j).wait_recv()
        block, q = place(j)
        q_out[j] = q.astype(BF16)
        q_copy(j).start()
        placed[j] = block.astype(BF16)

    for j in others:
        params_copy(j).wait_recv()
        slope_in = dot(fwd_params[j], mix2[:p_size], 0, 0)
        z = mixed(placed[j].astype(F32) / (1.0 + jnp.exp(-slope_in)), False)
        z_out[j] = z.astype(BF16)
        z_copy(j).start()

    gram_hi, gram_lo = halves(dot(basis[...], basis[...], 1, 1))

    def through_gram(x):
        return (dot(x, gram_hi, 1, 0) + dot(x, gram_lo, 1, 0)) * share

    block_own, q_own = place(mid)
    logits = dot(params, mixing, 0, 0, HIGH)
    decay = jnp.exp(-jnp.abs(logits))
    amps = jnp.maximum(logits, 0.0) + jnp.log1p(decay)
    slope = jnp.where(logits >= 0, 1.0, decay) / (1.0 + decay)
    out = mixed((through_gram(amps.astype(BF16)) - block_own) * slope)

    for copy in rim_copies:
        copy.wait_recv()
    masks = (dec > 0, dec < nd - 1, None, None)
    light = jnp.zeros_like(rim_out)
    for side in range(4):
        part = dot(blend_ref[side], rim_in[side], 1, 0, HIGH)
        light = light + (part if masks[side] is None else jnp.where(masks[side], part, 0.0))
    rim_before = through_gram(rim_out[...].astype(BF16))
    rim_grad = through_gram((rim_out[...] + light).astype(BF16))
    rim_slope = jnp.where(rim_logits >= 0, 1.0, rim_decay) / (1.0 + rim_decay)
    w = mixed((rim_grad - rim_before) * rim_slope)
    rim_grad = rim_grad - q_own
    slopes = [1.0 - jnp.exp(-rim_in[side]) for side in range(4)]

    for j in others:
        q_copy(j).wait_recv()
        rim_grad = rim_grad - q_in[j].astype(F32)

    w_copies = [
        remote(w_out.at[side], w_in.at[side], w_ssem.at[side], w_rsem.at[side], where)
        for side, where in enumerate((at_dec(-1), at_dec(1), at_ra(-1), at_ra(1)))
    ]
    for side in (2, 3, 0, 1):
        toward = dot(blend_ref[side], rim_grad, 0, 0, HIGH)
        w_out[side] = mixed(toward * slopes[side])
        w_copies[side].start()

    for j in others:
        z_copy(j).wait_recv()
        out = out - z_in[j].astype(F32)

    for copy in w_copies:
        copy.wait_recv()
    w = w + (
        jnp.where(dec < nd - 1, w_in[0], 0.0) + jnp.where(dec > 0, w_in[1], 0.0) + w_in[2] + w_in[3]
    )
    w_hi, w_lo = halves(w)
    out_ref[:, 0, :] = out + (dot(w_hi, pick, 1, 1) + dot(w_lo, pick, 1, 1))
    for copy in rim_copies + w_copies:
        copy.wait_send()
    for j in others:
        for copy in (slots_copy(j), params_copy(j), q_copy(j), z_copy(j)):
            copy.wait_send()


def local(params, mixing, basis, blend, border_ids, intersection, observed):
    p_size, rows = params.shape[1:]
    k = mixing.shape[1]
    noff, cap, pix = observed.shape[1:]
    border = border_ids.shape[1]
    top = intersection.shape[2]
    half = -(-p_size // 16) * 16
    wide = -(-(rows + border) // 128) * 128
    hbm = pl.BlockSpec(memory_space=pltpu.HBM)
    vmem = pltpu.VMEM
    dma = pltpu.SemaphoreType.DMA
    out = pl.pallas_call(
        kernel,
        out_shape=jax.ShapeDtypeStruct((p_size, 1, rows), F32),
        in_specs=[hbm] * 7,
        out_specs=pl.BlockSpec(memory_space=pltpu.VMEM),
        scratch_shapes=[
            vmem((p_size, rows), F32),
            vmem((p_size, k), F32),
            vmem((4, border, border), F32),
            vmem((1, border), jnp.int32),
            vmem((top, rows), jnp.int32),
            vmem((2 * half, k), BF16),
            vmem((noff, p_size, rows), BF16),
            vmem((noff, 8, wide), F32),
            vmem((noff, cap, pix), BF16),
            vmem((k, pix), BF16),
            vmem((noff, cap, k), BF16),
            vmem((noff, rows, k), BF16),
            vmem((noff, border, k), BF16),
            vmem((noff, border, k), BF16),
            vmem((noff, p_size, rows), BF16),
            vmem((noff, p_size, rows), BF16),
            vmem((border, k), F32),
            vmem((4, border, k), F32),
            vmem((4, p_size, border), F32),
            vmem((4, p_size, border), F32),
            dma((5,)), dma((noff,)), dma,
            dma((noff,)), dma((noff,)), dma((noff,)), dma((noff,)),
            dma((noff,)), dma((noff,)), dma((noff,)), dma((noff,)),
            dma((4,)), dma((4,)), dma((4,)), dma((4,)),
        ],
        compiler_params=pltpu.CompilerParams(
            collective_id=0, has_side_effects=True, vmem_limit_bytes=67043328 - 80 * 1024
        ),
        name="tiles",
    )(jnp.swapaxes(params, 0, 1), mixing, blend[0], border_ids, intersection[0].T, basis, observed[0])
    return jnp.swapaxes(out, 0, 1)


def solution(mesh):
    in_specs = (
        P(("dec", "ra"), None, None),
        P(),
        P(),
        P(("dec", "ra"), None, None, None),
        P(("dec", "ra"), None),
        P(("dec", "ra"), None, None),
        P(("dec", "ra"), None, None, None),
    )
    out_specs = P(("dec", "ra"), None, None)
    return jax.shard_map(local, mesh=mesh, in_specs=in_specs, out_specs=out_specs, check_vma=False)
```

```python
import math

import jax
import jax.numpy as jnp
from jax import lax
from jax.experimental import pallas as pl
from jax.experimental.pallas import tpu as pltpu
from jax.sharding import PartitionSpec as P

HIGH = lax.Precision.HIGHEST
MESH = pl.DeviceIdType.MESH
F32, BF16 = jnp.float32, jnp.bfloat16


def dot(a, b, da, db, precision=None):
    return lax.dot_general(
        a, b, (((da,), (db,)), ((), ())), precision=precision, preferred_element_type=F32
    )


def halves(x):
    high = x.astype(BF16)
    return high, (x - high.astype(F32)).astype(BF16)


def onehot(hit):
    return hit.astype(F32).astype(BF16)


def kernel(
    params_hbm, mixing_hbm, blend_hbm, ids_hbm, owners_hbm, basis_hbm, seen_hbm, out_ref,
    params_ref, mixing_ref, blend_ref, ids_ref, owners_ref, mix2, fwd_params, slots_out, slots_in,
    seen, basis, packed, placed, q_out, q_in, z_out, z_in, rim_out, rim_in, w_out, w_in,
    side_in, side_blend,
    in_sem, seen_sem, basis_sem, slots_ssem, slots_rsem, params_ssem, params_rsem,
    q_ssem, q_rsem, z_ssem, z_rsem, rim_ssem, rim_rsem, w_ssem, w_rsem,
    side_ssem, side_rsem, blend_ssem, blend_rsem,
):
    noff, cap, pix = seen.shape
    mid = noff // 2
    top, rows = owners_ref.shape
    border = ids_ref.shape[1]
    p_size = params_ref.shape[0]
    half = mix2.shape[0] // 2
    scale = 1.0 / math.sqrt(pix)
    share = top * scale
    nd, nr = lax.axis_size("dec"), lax.axis_size("ra")
    dec, ra = lax.axis_index("dec"), lax.axis_index("ra")
    others = [j for j in range(noff) if j != mid]

    def at_ra(step):
        return (dec, lax.rem(ra + step + nr, nr))

    def at_dec(step):
        return (lax.rem(dec + step + nd, nd), ra)

    def turn(step):
        return jnp.where(step < mid, step, jnp.where(step < noff - 1, step + 1, mid))

    def seen_copy(j):
        return pltpu.make_async_copy(seen_hbm.at[j], seen.at[j], seen_sem.at[j])

    def remote(src, dst, ssem, rsem, where):
        return pltpu.make_async_remote_copy(
            src_ref=src, dst_ref=dst, send_sem=ssem, recv_sem=rsem,
            device_id=where, device_id_type=MESH,
        )

    def slots_copy(j):
        return remote(
            slots_out.at[j], slots_in.at[j], slots_ssem.at[j], slots_rsem.at[j], at_ra(j - mid)
        )

    def params_copy(j):
        return remote(
            fwd_params.at[mid], fwd_params.at[j], params_ssem.at[j], params_rsem.at[j], at_ra(j - mid)
        )

    def q_copy(j):
        return remote(q_out.at[j], q_in.at[j], q_ssem.at[j], q_rsem.at[j], at_ra(mid - j))

    def z_copy(j):
        return remote(z_out.at[j], z_in.at[j], z_ssem.at[j], z_rsem.at[j], at_ra(mid - j))

    def side_copy(n):
        return remote(
            q_out.at[(noff - 1, 0)[n]], side_in.at[n], side_ssem.at[n], side_rsem.at[n], at_ra((-1, 1)[n])
        )

    def blend_copy(n):
        return remote(
            blend_ref.at[3 - n], side_blend.at[n], blend_ssem.at[n], blend_rsem.at[n], at_ra((1, -1)[n])
        )

    def mixed(x, full=True):
        high, low = halves(x)
        both = dot(mix2[...], high, 1, 1)
        out = both[:p_size] + both[half : half + p_size]
        return out + dot(mix2[:half], low, 1, 1)[:p_size] if full else out

    in_copies = [
        pltpu.make_async_copy(src, dst, in_sem.at[n])
        for n, (src, dst) in enumerate((
            (ids_hbm, ids_ref), (owners_hbm, owners_ref), (params_hbm.at[:, 0, :], params_ref),
            (mixing_hbm, mixing_ref), (blend_hbm, blend_ref),
        ))
    ]
    for copy in in_copies:
        copy.start()
    basis_copy = pltpu.make_async_copy(basis_hbm, basis, basis_sem)
    basis_copy.start()
    seen_copy(0).start()

    barrier = pltpu.get_barrier_semaphore()
    peers = [at_dec(1), at_dec(-1)] + [at_ra(j - mid) for j in others]
    for peer in peers:
        pl.semaphore_signal(barrier, inc=1, device_id=peer, device_id_type=MESH)

    earlier = onehot(
        lax.broadcasted_iota(jnp.int32, (rows, rows), 0)
        < lax.broadcasted_iota(jnp.int32, (rows, rows), 1)
    )
    for copy in in_copies[:2]:
        copy.wait()
    pick = onehot(lax.broadcasted_iota(jnp.int32, (rows, border), 0) == ids_ref[...])
    spare = noff * (noff - 1) // 2 - jnp.sum(owners_ref[...], axis=0, keepdims=True)
    member = spare != lax.broadcasted_iota(jnp.int32, (8, rows), 0)
    slots = jnp.where(member, dot(onehot(member), earlier, 1, 0), -1.0)
    slots_hi, slots_lo = halves(slots)
    rim_slots = dot(slots_hi, pick, 1, 0) + dot(slots_lo, pick, 1, 0)
    slots_out[...] = jnp.full(slots_out.shape, -1.0, F32)
    for j in range(noff):
        slots_out[j, :, :rows] = slots[j : j + 1]
        slots_out[j, :, rows : rows + border] = rim_slots[j : j + 1]
    pl.semaphore_wait(barrier, len(peers))
    for j in others:
        slots_copy(j).start()
    mix2[...] = jnp.zeros_like(mix2)
    for copy in in_copies[2:]:
        copy.wait()
    seen_copy(1).start()
    params = params_ref[...]
    mixing = mixing_ref[...]
    mix_hi, mix_lo = halves(mixing)
    mix2[:p_size] = mix_hi
    mix2[half : half + p_size] = mix_lo
    fwd_params[mid] = params.astype(BF16)
    rim_params = dot(params, pick.astype(F32), 1, 0, HIGH)
    rim_logits = dot(rim_params, mixing, 0, 0, HIGH)
    rim_decay = jnp.exp(-jnp.abs(rim_logits))
    rim_out[...] = jnp.maximum(rim_logits, 0.0) + jnp.log1p(rim_decay)
    for j in others:
        params_copy(j).start()
    rim_copies = [
        remote(rim_out, rim_in.at[slot], rim_ssem.at[slot], rim_rsem.at[slot], where)
        for slot, where in enumerate((at_dec(1), at_dec(-1), at_ra(1), at_ra(-1)))
    ]
    for copy in rim_copies:
        copy.start()
    for n in range(2):
        blend_copy(n).start()

    basis_copy.wait()

    def render(step, carry):
        j = turn(step)
        seen_copy(j).wait()

        @pl.when(step + 2 < noff)
        def _():
            seen_copy(turn(step + 2)).start()

        packed[j] = (dot(seen[j], basis[...], 1, 1) * scale).astype(BF16)
        return carry

    lax.fori_loop(0, noff, render, 0)

    places = lax.broadcasted_iota(jnp.int32, (rows + border, cap), 1).astype(F32)

    def place(row):
        column = jnp.broadcast_to(row, (8, row.shape[1])).T[: rows + border, :1]
        return column

    def split(column, j):
        block = dot(onehot(column == places), packed[j], 1, 0)
        return block[:rows], block[rows:]

    for j in others:
        slots_copy(j).wait_recv()
        block, q = split(place(slots_in[j]), j)
        q_out[j] = q.astype(BF16)
        q_copy(j).start()
        if j in (0, noff - 1):
            side_copy(0 if j else 1).start()
        placed[j] = block.astype(BF16)

    for j in others:
        params_copy(j).wait_recv()
        slope_in = dot(fwd_params[j], mix2[:p_size], 0, 0)
        z = mixed(placed[j].astype(F32) / (1.0 + jnp.exp(-slope_in)), False)
        z_out[j] = z.astype(BF16)
        z_copy(j).start()

    gram_hi, gram_lo = halves(dot(basis[...], basis[...], 1, 1))

    def through_gram(x):
        return (dot(x, gram_hi, 1, 0) + dot(x, gram_lo, 1, 0)) * share

    block_own, q_own = split(place(slots_out[mid]), mid)

    for copy in rim_copies:
        copy.wait_recv()
    masks = (dec > 0, dec < nd - 1, None, None)
    light = jnp.zeros(rim_out.shape, F32)
    for side in range(4):
        part = dot(blend_ref[side], rim_in[side], 1, 0, HIGH)
        light = light + (part if masks[side] is None else jnp.where(masks[side], part, 0.0))
    rim_own = through_gram((rim_out[...] + light).astype(BF16))
    rim_grad = rim_own - q_own
    w_copies = [
        remote(w_out.at[side], w_in.at[side], w_ssem.at[side], w_rsem.at[side], where)
        for side, where in enumerate((at_dec(-1), at_dec(1), at_ra(-1), at_ra(1)))
    ]

    def tell(side, grad):
        slope = 1.0 - jnp.exp(-rim_in[side])
        w_out[side] = mixed(dot(blend_ref[side], grad, 0, 0, HIGH) * slope)
        w_copies[side].start()

    for j in range(mid):
        q_copy(j).wait_recv()
    from_west = q_in[0].astype(F32) + q_in[1].astype(F32)
    tell(3, rim_grad - from_west)
    for j in range(mid + 1, noff):
        q_copy(j).wait_recv()
    from_east = q_in[mid + 1].astype(F32) + q_in[noff - 1].astype(F32)
    tell(2, rim_grad - from_east)
    rim_grad = rim_grad - from_west - from_east
    for side in range(2):
        tell(side, rim_grad)

    logits = dot(params, mixing, 0, 0, HIGH)
    decay = jnp.exp(-jnp.abs(logits))
    amps = jnp.maximum(logits, 0.0) + jnp.log1p(decay)
    slope = jnp.where(logits >= 0, 1.0, decay) / (1.0 + decay)
    out = mixed((through_gram(amps.astype(BF16)) - block_own) * slope)
    rim_slope = jnp.where(rim_logits >= 0, 1.0, rim_decay) / (1.0 + rim_decay)
    gained = rim_own - through_gram(rim_out[...].astype(BF16))
    for n in range(2):
        blend_copy(n).wait_recv()
        side_copy(n).wait_recv()
        heard = q_out[(mid + 1, mid - 1)[n]].astype(F32) + side_in[n].astype(F32)
        gained = gained - dot(side_blend[n], heard, 0, 0, HIGH)
    w = mixed(gained * rim_slope)

    for j in others:
        z_copy(j).wait_recv()
        out = out - z_in[j].astype(F32)

    for copy in w_copies:
        copy.wait_recv()
    w = w + (
        jnp.where(dec < nd - 1, w_in[0], 0.0) + jnp.where(dec > 0, w_in[1], 0.0) + w_in[2] + w_in[3]
    )
    w_hi, w_lo = halves(w)
    out_ref[:, 0, :] = out + (dot(w_hi, pick, 1, 1) + dot(w_lo, pick, 1, 1))
    for copy in rim_copies + w_copies:
        copy.wait_send()
    for j in others:
        for copy in (slots_copy(j), params_copy(j), q_copy(j), z_copy(j)):
            copy.wait_send()
    for n in range(2):
        side_copy(n).wait_send()
        blend_copy(n).wait_send()


def local(params, mixing, basis, blend, border_ids, intersection, observed):
    p_size, rows = params.shape[1:]
    k = mixing.shape[1]
    noff, cap, pix = observed.shape[1:]
    border = border_ids.shape[1]
    top = intersection.shape[2]
    half = -(-p_size // 16) * 16
    wide = -(-(rows + border) // 128) * 128
    hbm = pl.BlockSpec(memory_space=pltpu.HBM)
    vmem = pltpu.VMEM
    dma = pltpu.SemaphoreType.DMA
    out = pl.pallas_call(
        kernel,
        out_shape=jax.ShapeDtypeStruct((p_size, 1, rows), F32),
        in_specs=[hbm] * 7,
        out_specs=pl.BlockSpec(memory_space=pltpu.VMEM),
        scratch_shapes=[
            vmem((p_size, rows), F32),
            vmem((p_size, k), F32),
            vmem((4, border, border), F32),
            vmem((1, border), jnp.int32),
            vmem((top, rows), jnp.int32),
            vmem((2 * half, k), BF16),
            vmem((noff, p_size, rows), BF16),
            vmem((noff, 1, wide), F32),
            vmem((noff, 1, wide), F32),
            vmem((noff, cap, pix), BF16),
            vmem((k, pix), BF16),
            vmem((noff, cap, k), BF16),
            vmem((noff, rows, k), BF16),
            vmem((noff, border, k), BF16),
            vmem((noff, border, k), BF16),
            vmem((noff, p_size, rows), BF16),
            vmem((noff, p_size, rows), BF16),
            vmem((border, k), F32),
            vmem((4, border, k), F32),
            vmem((4, p_size, border), F32),
            vmem((4, p_size, border), F32),
            vmem((2, border, k), BF16),
            vmem((2, border, border), F32),
            dma((5,)), dma((noff,)), dma,
            dma((noff,)), dma((noff,)), dma((noff,)), dma((noff,)),
            dma((noff,)), dma((noff,)), dma((noff,)), dma((noff,)),
            dma((4,)), dma((4,)), dma((4,)), dma((4,)),
            dma((2,)), dma((2,)), dma((2,)), dma((2,)),
        ],
        compiler_params=pltpu.CompilerParams(
            collective_id=0, has_side_effects=True, vmem_limit_bytes=48 * 1024 * 1024
        ),
        name="tiles",
    )(*[
        pltpu.with_memory_space_constraint(x, pltpu.HBM)
        for x in (
            jnp.swapaxes(params, 0, 1), mixing, blend[0], border_ids, intersection[0].T, basis, observed[0],
        )
    ])
    return jnp.swapaxes(out, 0, 1)


def solution(mesh):
    in_specs = (
        P(("dec", "ra"), None, None),
        P(),
        P(),
        P(("dec", "ra"), None, None, None),
        P(("dec", "ra"), None),
        P(("dec", "ra"), None, None),
        P(("dec", "ra"), None, None, None),
    )
    out_specs = P(("dec", "ra"), None, None)
    return jax.shard_map(local, mesh=mesh, in_specs=in_specs, out_specs=out_specs, check_vma=False)
```

```python
import math

import jax
import jax.numpy as jnp
from jax import lax
from jax.experimental import pallas as pl
from jax.experimental.pallas import tpu as pltpu
from jax.sharding import PartitionSpec as P

HIGH = lax.Precision.HIGHEST
MESH = pl.DeviceIdType.MESH
F32, BF16 = jnp.float32, jnp.bfloat16


def dot(a, b, da, db, precision=None):
    return lax.dot_general(
        a, b, (((da,), (db,)), ((), ())), precision=precision, preferred_element_type=F32
    )


def halves(x):
    high = x.astype(BF16)
    return high, (x - high.astype(F32)).astype(BF16)


def onehot(hit):
    return hit.astype(F32).astype(BF16)


def kernel(
    params_hbm, mixing_hbm, blend_hbm, ids_hbm, owners_hbm, basis_hbm, seen_hbm, out_ref,
    params_ref, mixing_ref, blend_ref, ids_ref, owners_ref, mix2, fwd_params, slots_out, slots_in,
    seen, basis, packed, placed, q_out, q_in, z_out, z_in, rim_out, rim_in, w_out, w_in,
    side_in, side_blend,
    in_sem, seen_sem, basis_sem, slots_ssem, slots_rsem, params_ssem, params_rsem,
    q_ssem, q_rsem, z_ssem, z_rsem, rim_ssem, rim_rsem, w_ssem, w_rsem,
    side_ssem, side_rsem, blend_ssem, blend_rsem,
):
    noff, cap, pix = seen.shape
    mid = noff // 2
    top, rows = owners_ref.shape
    border = ids_ref.shape[1]
    p_size = params_ref.shape[0]
    half = mix2.shape[0] // 2
    scale = 1.0 / math.sqrt(pix)
    share = top * scale
    nd, nr = lax.axis_size("dec"), lax.axis_size("ra")
    dec, ra = lax.axis_index("dec"), lax.axis_index("ra")
    others = [j for j in range(noff) if j != mid]

    def at_ra(step):
        return (dec, lax.rem(ra + step + nr, nr))

    def at_dec(step):
        return (lax.rem(dec + step + nd, nd), ra)

    def turn(step):
        return jnp.where(step < mid, step, jnp.where(step < noff - 1, step + 1, mid))

    def seen_copy(j):
        return pltpu.make_async_copy(seen_hbm.at[j], seen.at[j], seen_sem.at[j])

    def remote(src, dst, ssem, rsem, where):
        return pltpu.make_async_remote_copy(
            src_ref=src, dst_ref=dst, send_sem=ssem, recv_sem=rsem,
            device_id=where, device_id_type=MESH,
        )

    def slots_copy(j):
        return remote(
            slots_out.at[j], slots_in.at[j], slots_ssem.at[j], slots_rsem.at[j], at_ra(j - mid)
        )

    def params_copy(j):
        return remote(
            fwd_params.at[mid], fwd_params.at[j], params_ssem.at[j], params_rsem.at[j], at_ra(j - mid)
        )

    def q_copy(j):
        return remote(q_out.at[j], q_in.at[j], q_ssem.at[j], q_rsem.at[j], at_ra(mid - j))

    def z_copy(j):
        return remote(z_out.at[j], z_in.at[j], z_ssem.at[j], z_rsem.at[j], at_ra(mid - j))

    def side_copy(n):
        return remote(
            q_out.at[(noff - 1, 0)[n]], side_in.at[n], side_ssem.at[n], side_rsem.at[n], at_ra((-1, 1)[n])
        )

    def blend_copy(n):
        return remote(
            blend_ref.at[3 - n], side_blend.at[n], blend_ssem.at[n], blend_rsem.at[n], at_ra((1, -1)[n])
        )

    def mixed(x, full=True):
        high, low = halves(x)
        both = dot(mix2[...], high, 1, 1)
        out = both[:p_size] + both[half : half + p_size]
        return out + dot(mix2[:half], low, 1, 1)[:p_size] if full else out

    in_copies = [
        pltpu.make_async_copy(src, dst, in_sem.at[n])
        for n, (src, dst) in enumerate((
            (ids_hbm, ids_ref), (owners_hbm, owners_ref), (params_hbm.at[:, 0, :], params_ref),
            (mixing_hbm, mixing_ref), (blend_hbm, blend_ref),
        ))
    ]
    for copy in in_copies:
        copy.start()
    basis_copy = pltpu.make_async_copy(basis_hbm, basis, basis_sem)
    basis_copy.start()
    seen_copy(0).start()

    barrier = pltpu.get_barrier_semaphore()
    peers = [at_dec(1), at_dec(-1)] + [at_ra(j - mid) for j in others]
    for peer in peers:
        pl.semaphore_signal(barrier, inc=1, device_id=peer, device_id_type=MESH)

    earlier = onehot(
        lax.broadcasted_iota(jnp.int32, (rows, rows), 0)
        < lax.broadcasted_iota(jnp.int32, (rows, rows), 1)
    )
    for copy in in_copies[:2]:
        copy.wait()
    pick = onehot(lax.broadcasted_iota(jnp.int32, (rows, border), 0) == ids_ref[...])
    spare = noff * (noff - 1) // 2 - jnp.sum(owners_ref[...], axis=0, keepdims=True)
    member = spare != lax.broadcasted_iota(jnp.int32, (8, rows), 0)
    slots = jnp.where(member, dot(onehot(member), earlier, 1, 0), -1.0)
    slots_hi, slots_lo = halves(slots)
    rim_slots = dot(slots_hi, pick, 1, 0) + dot(slots_lo, pick, 1, 0)
    slots_out[...] = jnp.full(slots_out.shape, -1.0, F32)
    for j in range(noff):
        slots_out[j, :, :rows] = slots[j : j + 1]
        slots_out[j, :, rows : rows + border] = rim_slots[j : j + 1]
    pl.semaphore_wait(barrier, len(peers))
    for j in others:
        slots_copy(j).start()
    mix2[...] = jnp.zeros_like(mix2)
    for copy in in_copies[2:]:
        copy.wait()
    seen_copy(1).start()
    params = params_ref[...]
    mixing = mixing_ref[...]
    mix_hi, mix_lo = halves(mixing)
    mix2[:p_size] = mix_hi
    mix2[half : half + p_size] = mix_lo
    fwd_params[mid] = params.astype(BF16)
    rim_params = dot(params, pick.astype(F32), 1, 0, HIGH)
    rim_logits = dot(rim_params, mixing, 0, 0, HIGH)
    rim_decay = jnp.exp(-jnp.abs(rim_logits))
    rim_out[...] = jnp.maximum(rim_logits, 0.0) + jnp.log1p(rim_decay)
    for j in others:
        params_copy(j).start()
    rim_copies = [
        remote(rim_out, rim_in.at[slot], rim_ssem.at[slot], rim_rsem.at[slot], where)
        for slot, where in enumerate((at_dec(1), at_dec(-1), at_ra(1), at_ra(-1)))
    ]
    for copy in rim_copies:
        copy.start()
    for n in range(2):
        blend_copy(n).start()

    basis_copy.wait()

    def render(step, carry):
        j = turn(step)
        seen_copy(j).wait()

        @pl.when(step + 2 < noff)
        def _():
            seen_copy(turn(step + 2)).start()

        packed[j] = (dot(seen[j], basis[...], 1, 1) * scale).astype(BF16)
        return carry

    lax.fori_loop(0, noff, render, 0)

    places = lax.broadcasted_iota(jnp.int32, (rows + border, cap), 1).astype(F32)

    def place(row):
        column = jnp.broadcast_to(row, (8, row.shape[1])).T[: rows + border, :1]
        return column

    def split(column, j):
        block = dot(onehot(column == places), packed[j], 1, 0)
        return block[:rows], block[rows:]

    for j in others:
        slots_copy(j).wait_recv()
        block, q = split(place(slots_in[j]), j)
        q_out[j] = q.astype(BF16)
        q_copy(j).start()
        if j in (0, noff - 1):
            side_copy(0 if j else 1).start()
        placed[j] = block.astype(BF16)

    gram_hi, gram_lo = halves(dot(basis[...], basis[...], 1, 1))

    def through_gram(x):
        return (dot(x, gram_hi, 1, 0) + dot(x, gram_lo, 1, 0)) * share

    block_own, q_own = split(place(slots_out[mid]), mid)

    for copy in rim_copies:
        copy.wait_recv()
    masks = (dec > 0, dec < nd - 1, None, None)
    light = jnp.zeros(rim_out.shape, F32)
    for side in range(4):
        part = dot(blend_ref[side], rim_in[side], 1, 0, HIGH)
        light = light + (part if masks[side] is None else jnp.where(masks[side], part, 0.0))
    rim_own = through_gram((rim_out[...] + light).astype(BF16))
    rim_grad = rim_own - q_own
    w_copies = [
        remote(w_out.at[side], w_in.at[side], w_ssem.at[side], w_rsem.at[side], where)
        for side, where in enumerate((at_dec(-1), at_dec(1), at_ra(-1), at_ra(1)))
    ]

    def tell(side, grad):
        slope = 1.0 - jnp.exp(-rim_in[side])
        w_out[side] = mixed(dot(blend_ref[side], grad, 0, 0, HIGH) * slope)
        w_copies[side].start()

    for j in others:
        params_copy(j).wait_recv()
        slope_in = dot(fwd_params[j], mix2[:p_size], 0, 0)
        z = mixed(placed[j].astype(F32) / (1.0 + jnp.exp(-slope_in)), False)
        z_out[j] = z.astype(BF16)
        z_copy(j).start()

    for j in range(mid):
        q_copy(j).wait_recv()
    from_west = q_in[0].astype(F32) + q_in[1].astype(F32)
    tell(3, rim_grad - from_west)
    for j in range(mid + 1, noff):
        q_copy(j).wait_recv()
    from_east = q_in[mid + 1].astype(F32) + q_in[noff - 1].astype(F32)
    for side in range(2):
        tell(side, rim_grad - from_west - from_east)
    tell(2, rim_grad - from_east)

    logits = dot(params, mixing, 0, 0, HIGH)
    decay = jnp.exp(-jnp.abs(logits))
    amps = jnp.maximum(logits, 0.0) + jnp.log1p(decay)
    slope = jnp.where(logits >= 0, 1.0, decay) / (1.0 + decay)
    out = mixed((through_gram(amps.astype(BF16)) - block_own) * slope)
    rim_slope = jnp.where(rim_logits >= 0, 1.0, rim_decay) / (1.0 + rim_decay)
    gained = rim_own - through_gram(rim_out[...].astype(BF16))
    for n in range(2):
        blend_copy(n).wait_recv()
        side_copy(n).wait_recv()
        heard = q_out[(mid + 1, mid - 1)[n]].astype(F32) + side_in[n].astype(F32)
        gained = gained - dot(side_blend[n], heard, 0, 0, HIGH)
    w = mixed(gained * rim_slope)

    for j in others:
        z_copy(j).wait_recv()
        out = out - z_in[j].astype(F32)

    for copy in w_copies:
        copy.wait_recv()
    w = w + (
        jnp.where(dec < nd - 1, w_in[0], 0.0) + jnp.where(dec > 0, w_in[1], 0.0) + w_in[2] + w_in[3]
    )
    w_hi, w_lo = halves(w)
    out_ref[:, 0, :] = out + (dot(w_hi, pick, 1, 1) + dot(w_lo, pick, 1, 1))
    for copy in rim_copies + w_copies:
        copy.wait_send()
    for j in others:
        for copy in (slots_copy(j), params_copy(j), q_copy(j), z_copy(j)):
            copy.wait_send()
    for n in range(2):
        side_copy(n).wait_send()
        blend_copy(n).wait_send()


def local(params, mixing, basis, blend, border_ids, intersection, observed):
    p_size, rows = params.shape[1:]
    k = mixing.shape[1]
    noff, cap, pix = observed.shape[1:]
    border = border_ids.shape[1]
    top = intersection.shape[2]
    half = -(-p_size // 16) * 16
    wide = -(-(rows + border) // 128) * 128
    hbm = pl.BlockSpec(memory_space=pltpu.HBM)
    vmem = pltpu.VMEM
    dma = pltpu.SemaphoreType.DMA
    out = pl.pallas_call(
        kernel,
        out_shape=jax.ShapeDtypeStruct((p_size, 1, rows), F32),
        in_specs=[hbm] * 7,
        out_specs=pl.BlockSpec(memory_space=pltpu.VMEM),
        scratch_shapes=[
            vmem((p_size, rows), F32),
            vmem((p_size, k), F32),
            vmem((4, border, border), F32),
            vmem((1, border), jnp.int32),
            vmem((top, rows), jnp.int32),
            vmem((2 * half, k), BF16),
            vmem((noff, p_size, rows), BF16),
            vmem((noff, 1, wide), F32),
            vmem((noff, 1, wide), F32),
            vmem((noff, cap, pix), BF16),
            vmem((k, pix), BF16),
            vmem((noff, cap, k), BF16),
            vmem((noff, rows, k), BF16),
            vmem((noff, border, k), BF16),
            vmem((noff, border, k), BF16),
            vmem((noff, p_size, rows), BF16),
            vmem((noff, p_size, rows), BF16),
            vmem((border, k), F32),
            vmem((4, border, k), F32),
            vmem((4, p_size, border), F32),
            vmem((4, p_size, border), F32),
            vmem((2, border, k), BF16),
            vmem((2, border, border), F32),
            dma((5,)), dma((noff,)), dma,
            dma((noff,)), dma((noff,)), dma((noff,)), dma((noff,)),
            dma((noff,)), dma((noff,)), dma((noff,)), dma((noff,)),
            dma((4,)), dma((4,)), dma((4,)), dma((4,)),
            dma((2,)), dma((2,)), dma((2,)), dma((2,)),
        ],
        compiler_params=pltpu.CompilerParams(
            collective_id=0, has_side_effects=True, vmem_limit_bytes=48 * 1024 * 1024
        ),
        name="tiles",
    )(*[
        pltpu.with_memory_space_constraint(x, pltpu.HBM)
        for x in (
            jnp.swapaxes(params, 0, 1), mixing, blend[0], border_ids, intersection[0].T, basis, observed[0],
        )
    ])
    return jnp.swapaxes(out, 0, 1)


def solution(mesh):
    in_specs = (
        P(("dec", "ra"), None, None),
        P(),
        P(),
        P(("dec", "ra"), None, None, None),
        P(("dec", "ra"), None),
        P(("dec", "ra"), None, None),
        P(("dec", "ra"), None, None, None),
    )
    out_specs = P(("dec", "ra"), None, None)
    return jax.shard_map(local, mesh=mesh, in_specs=in_specs, out_specs=out_specs, check_vma=False)
```
